768 devices in a mesh: section: 24 (over x_lo, z), row: 8 (over y), col: 4 (over x_hi, core).
Axes of the slice: x: 4 (x_hi: 2, x_lo: 2; x = x_hi * 2 + x_lo), y: 8, z: 12, core: 2. Of those that a mesh axis runs over, the one named last changes fastest.
Arguments:
- upstream: bfloat16 [24, 6144, 512], P('section', ('row', 'col')), may hold values from -6 to 6
- attended: bfloat16 [24, 3072, 1024], P('section', 'col'), may hold values from -0.75 to 0.75
- weight: bfloat16 [24, 6144, 3072], P('section', 'row', 'col'), may hold values from -0.078125 to 0.078125
Outputs:
- attended_grad: bfloat16 [24, 3072, 1024], P('section', ('col', 'row'))
- weight_grad: bfloat16 [24, 6144, 3072], P('section', 'row', 'col')
The draws below stay inside these ranges and needn't reach their ends.
All inputs are finite; a program needn't handle non-finite values.
Results may differ from the reference program's by a relative error of at most 0.001.
Values may be sent and summed in bfloat16 or wider, within the bound.
A program may use at most 32 MiB of HBM per device.

```python
import jax
import jax.numpy as jnp
from jax import lax

D = 6144
TOK = 1024
SECTIONS = 12
AF = 6144
N_SECTION = 24


def steps_of(stream_key, shape, split, smallest, high):
    factor_of, own = 1.0, jax.random.fold_in(stream_key, 6)
    for position, parts in split:
        steps = jnp.exp(jax.random.uniform(jax.random.fold_in(own, position), (parts,), jnp.float32, smallest / len(split), high / len(split)))
        factor_of = factor_of * jnp.repeat(steps, shape[position] // parts).reshape([-1 if axis == position else 1 for axis in range(len(shape))])
    return factor_of


def gaussian(key, shape, width, reach, split=(), dtype=jnp.bfloat16):
    result = jax.random.normal(key, shape, jnp.float32) * width
    if len(split) > 0:
        result = steps_of(key, shape, split, -0.22, 0.18) * result
    return jnp.clip(result, min=-reach, max=reach).astype(dtype)


def setup_inputs(seed: int = 0) -> dict:
    arg_keys = jax.random.split(jax.random.key(seed), 4)
    upstream = gaussian(arg_keys[0], (N_SECTION, D, TOK // 2), 1.0, 6.0, ((0, 24), (1, 32)))
    attended = gaussian(arg_keys[1], (N_SECTION, AF // 2, TOK), 0.125, 0.75, ((0, 24), (1, 4)))
    weight = gaussian(arg_keys[2], (N_SECTION, D, AF // 2), D ** -0.5, 0.078125, ((0, 24), (1, 8), (2, 4)))
    return dict(upstream=upstream, attended=attended, weight=weight)


def per_entry(operands):
    grad_rows, attn_rows, weight_cols = operands
    attn_grad = jnp.dot(weight_cols.T, grad_rows, preferred_element_type=jnp.float32).astype(jnp.bfloat16)
    proj_grad = jnp.dot(grad_rows, attn_rows.T, preferred_element_type=jnp.float32).astype(jnp.bfloat16)
    return attn_grad, proj_grad


def reference(upstream, attended, weight):
    arriving = jnp.roll(upstream, -1, axis=0)
    section_grads = jnp.concatenate([arriving[:SECTIONS], arriving[SECTIONS:]], axis=2)
    entry_grads = jnp.concatenate([section_grads, section_grads], axis=0)
    attended_grad, weight_grad = lax.map(per_entry, (entry_grads, attended, weight))
    return attended_grad, weight_grad
```

```python
import functools

import jax
import jax.numpy as jnp
from jax import lax
from jax.experimental import pallas as pl
from jax.experimental.pallas import tpu as pltpu
from jax.sharding import PartitionSpec as P

MESH = pl.DeviceIdType.MESH
CHUNKS = 4
ROWS = 8
OTHER = 4


def kernel(
    chips_z, up, attended, weight, ag_out, wg_out,
    panel, att, w, w_t, part, arrived, wg, ag,
    load_sem, store_sem, g_send, g_recv, r_send, r_recv,
):
    section, row, col = lax.axis_index("section"), lax.axis_index("row"), lax.axis_index("col")
    x_lo, z = section // chips_z, section % chips_z
    x_hi, core = col // 2, col % 2
    x = 2 * x_hi + x_lo
    width = panel.shape[-1]
    tokens = up.shape[-1]
    share = ag.shape[0]

    def at(x_pos, z_pos, core_pos, row_pos):
        return ((x_pos % 2) * chips_z + z_pos, row_pos, (x_pos // 2) * 2 + core_pos)

    z_before = (z + chips_z - 1) % chips_z
    z_after = (z + 1) % chips_z
    x_right, x_left, x_far = (x + 1) % 4, (x + 3) % 4, (x + 2) % 4
    below = at(x, z_before, core, row)
    above = at(x, z_after, core, row)
    right, left = at(x_right, z, core, row), at(x_left, z, core, row)
    sibling = at(x, z, 1 - core, row)
    up_row, down_row = at(x, z, core, (row + 1) % ROWS), at(x, z, core, (row + ROWS - 1) % ROWS)

    barrier = pltpu.get_barrier_semaphore()
    for other in (below, above, right, left, sibling, up_row, down_row):
        pl.semaphore_signal(barrier, inc=1, device_id=other, device_id_type=MESH)
    load_w = pltpu.make_async_copy(weight.at[0], w, load_sem.at[0])
    load_a = pltpu.make_async_copy(attended.at[0], att, load_sem.at[1])
    load_w.start()
    load_a.start()
    pl.semaphore_wait(barrier, 7)

    wrapped = (z + 1) // chips_z

    def slot(q, x_pos, core_pos):
        half = (x_pos % 2 + wrapped) % 2
        return panel.at[q, half, (x_pos // 2) * 2 + core_pos]

    def gather_copy(q, src, dst, send, recv, device):
        return pltpu.make_async_remote_copy(
            src_ref=src, dst_ref=dst, send_sem=g_send.at[q, send], recv_sem=g_recv.at[q, recv],
            device_id=device, device_id_type=MESH,
        )

    pending = []

    def send(q, src, dst, send_index, recv_index, device):
        copy = gather_copy(q, src, dst, send_index, recv_index, device)
        copy.start()
        pending.append(copy)

    sources = (x, x_left, x_right, x_far)

    def arrival(q, index):
        core_pos = core if index < OTHER else 1 - core
        place = slot(q, sources[index % OTHER], core_pos)
        gather_copy(q, place, place, 0, index, sibling).wait_recv()
        return place

    send_wrap = 1 - (z + chips_z - 1) // chips_z
    for q in range(CHUNKS):
        half = (x_lo + send_wrap) % 2
        send(q, up.at[0, :, pl.ds(q * width, width)], panel.at[q, half, col], 0, 0, below)

    load_w.wait()
    w_t[...] = w[...].T

    def own(q):
        place = arrival(q, 0)
        send(q, place, place, 1, 1, right)
        send(q, place, place, 2, 2, left)
        send(q, place, place, 3, OTHER, sibling)

    def near(q):
        from_left = arrival(q, 1)
        if q % 2 == 0:
            send(q, from_left, from_left, 7, 3, right)
        send(q, from_left, from_left, 4, OTHER + 1, sibling)
        from_right = arrival(q, 2)
        if q % 2 == 1:
            send(q, from_right, from_right, 7, 3, left)
        send(q, from_right, from_right, 5, OTHER + 2, sibling)

    def far(q):
        place = arrival(q, 3)
        send(q, place, place, 6, OTHER + 3, sibling)

    ways = (up_row, down_row)

    def ring_copy(q, way, half, step):
        ahead = OTHER - step
        dest = (row + (ahead if way == 0 else ROWS - ahead)) % ROWS
        return pltpu.make_async_remote_copy(
            src_ref=part.at[q, dest, half], dst_ref=arrived.at[q, way, step, half],
            send_sem=r_send.at[q, way, half, step], recv_sem=r_recv.at[q, way, half, step],
            device_id=ways[way], device_id_type=MESH,
        )

    def ring_send(q, way, half, step):
        copy = ring_copy(q, way, half, step)
        copy.start()
        pending.append(copy)

    def ring_start(q):
        for index in range(OTHER, 2 * OTHER):
            arrival(q, index)
        rows = panel.shape[2] * panel.shape[3]
        both = jnp.concatenate([panel[q, half].reshape(rows, width) for half in range(2)], axis=1)
        product = jnp.dot(w_t[...], both, preferred_element_type=jnp.float32)
        for half in range(2):
            part[q, :, half] = product[:, half * width:(half + 1) * width].reshape(ROWS, share, width)
        ring_send(q, 0, 0, 0)
        ring_send(q, 1, 1, 0)
        ring_send(q, 0, 1, 1)
        ring_send(q, 1, 0, 1)

    def ring_step(q, step):
        for half in range(2):
            for way in range(2):
                way = (way + half) % 2
                if step == 0 and way != half:
                    continue
                ring_copy(q, way, half, step).wait_recv()
                ahead = 3 - step
                dest = (row + (ahead if way == 0 else ROWS - ahead)) % ROWS
                if step < 3:
                    part[q, dest, half] += arrived[q, way, step, half]
                    ring_send(q, way, half, step + 1)
            if step == 3:
                total = part[q, row, half] + arrived[q, 0, 3, half] + arrived[q, 1, 3, half]
                begin = half * tokens + q * width
                ag[:, begin:begin + width] = total.astype(ag.dtype)

    stores = []

    def weight_grad(block):
        if block == 0:
            load_a.wait()
        lines = jnp.concatenate(
            [panel[q, half, block] for half in range(2) for q in range(CHUNKS)], axis=1
        )
        result = lax.dot_general(
            lines, att[...], (((1,), (1,)), ((), ())), preferred_element_type=jnp.float32
        )
        count = panel.shape[3]
        wg[pl.ds(block * count, count), :] = result.astype(wg.dtype)
        store = pltpu.make_async_copy(
            wg.at[pl.ds(block * count, count), :], wg_out.at[0, pl.ds(block * count, count), :],
            store_sem.at[block],
        )
        store.start()
        stores.append(store)

    own(0)
    own(1)
    near(0)
    own(2)
    far(0)
    near(1)
    own(3)
    ring_start(0)
    far(1)
    near(2)
    ring_start(1)
    far(2)
    near(3)
    ring_step(0, 0)
    ring_start(2)
    far(3)
    ring_step(1, 0)
    ring_start(3)
    ring_step(2, 0)
    weight_grad(0)
    ring_step(3, 0)
    ring_step(0, 1)
    weight_grad(1)
    ring_step(1, 1)
    ring_step(2, 1)
    weight_grad(2)
    ring_step(3, 1)
    ring_step(0, 2)
    weight_grad(3)
    for q in range(1, CHUNKS):
        ring_step(q, 2)
    for q in range(CHUNKS):
        ring_step(q, 3)
    store = pltpu.make_async_copy(ag, ag_out.at[0], store_sem.at[4])
    store.start()
    stores.append(store)
    for copy in pending:
        copy.wait_send()
    for store in stores:
        store.wait()


def on_device(chips_z, upstream, attended, weight):
    _, lines, tokens = upstream.shape
    _, features, all_tokens = attended.shape
    _, rows, _ = weight.shape
    share = features // ROWS
    width = tokens // CHUNKS
    bf16 = jnp.bfloat16
    dma = pltpu.SemaphoreType.DMA
    return pl.pallas_call(
        functools.partial(kernel, chips_z),
        out_shape=(
            jax.ShapeDtypeStruct((1, share, all_tokens), bf16),
            jax.ShapeDtypeStruct((1, rows, features), bf16),
        ),
        in_specs=[pl.BlockSpec(memory_space=pl.ANY)] * 3,
        out_specs=[pl.BlockSpec(memory_space=pl.ANY)] * 2,
        scratch_shapes=[
            pltpu.VMEM((CHUNKS, 2, rows // lines, lines, width), bf16),
            pltpu.VMEM((features, all_tokens), bf16),
            pltpu.VMEM((rows, features), bf16),
            pltpu.VMEM((features, rows), bf16),
            pltpu.VMEM((CHUNKS, ROWS, 2, share, width), jnp.float32),
            pltpu.VMEM((CHUNKS, 2, 4, 2, share, width), jnp.float32),
            pltpu.VMEM((rows, features), bf16),
            pltpu.VMEM((share, all_tokens), bf16),
            dma((2,)),
            dma((5,)),
            dma((CHUNKS, 8)),
            dma((CHUNKS, 8)),
            dma((CHUNKS, 2, 2, 4)),
            dma((CHUNKS, 2, 2, 4)),
        ],
        compiler_params=pltpu.CompilerParams(collective_id=0, has_side_effects=True),
    )(upstream, attended, weight)


def solution(mesh):
    placed = (
        P("section", ("row", "col"), None),
        P("section", "col", None),
        P("section", "row", "col"),
    )
    return jax.shard_map(
        functools.partial(on_device, mesh.shape["section"] // 2),
        mesh=mesh,
        in_specs=placed,
        out_specs=(P("section", ("col", "row"), None), P("section", "row", "col")),
        check_vma=False,
    )
```

```python
import functools

import jax
import jax.numpy as jnp
from jax import lax
from jax.experimental import pallas as pl
from jax.experimental.pallas import tpu as pltpu
from jax.sharding import PartitionSpec as P

MESH = pl.DeviceIdType.MESH
CHUNKS = 4
ROWS = 8
OTHER = 4


def kernel(
    chips_z, up, attended, weight, ag, wg,
    panel, att, w, w_t, far_w, part, arrived,
    load_sem, w_send, w_recv, g_send, g_recv, r_send, r_recv,
):
    section, row, col = lax.axis_index("section"), lax.axis_index("row"), lax.axis_index("col")
    x_lo, z = section // chips_z, section % chips_z
    x_hi, core = col // 2, col % 2
    x = 2 * x_hi + x_lo
    width = panel.shape[-1]
    tokens = up.shape[-1]
    share, rows = w_t.shape[1:]

    def at(x_pos, z_pos, core_pos, row_pos):
        return ((x_pos % 2) * chips_z + z_pos, row_pos, (x_pos // 2) * 2 + core_pos)

    x_right, x_left, x_far = (x + 1) % 4, (x + 3) % 4, (x + 2) % 4
    below = at(x, (z + chips_z - 1) % chips_z, core, row)
    above = at(x, (z + 1) % chips_z, core, row)
    right, left = at(x_right, z, core, row), at(x_left, z, core, row)
    sibling = at(x, z, 1 - core, row)
    ways = at(x, z, core, (row + 1) % ROWS), at(x, z, core, (row + ROWS - 1) % ROWS)

    barrier = pltpu.get_barrier_semaphore()
    for other in (below, above, right, left, sibling, *ways):
        pl.semaphore_signal(barrier, inc=1, device_id=other, device_id_type=MESH)
    load_w = pltpu.make_async_copy(weight.at[0], w, load_sem.at[0])
    load_a = pltpu.make_async_copy(attended.at[0], att, load_sem.at[1])
    load_w.start()
    load_a.start()
    pl.semaphore_wait(barrier, 7)

    pending = []

    def remote(src, dst, send_sem, recv_sem, device):
        return pltpu.make_async_remote_copy(
            src_ref=src, dst_ref=dst, send_sem=send_sem, recv_sem=recv_sem,
            device_id=device, device_id_type=MESH,
        )

    def start(copy):
        copy.start()
        pending.append(copy)

    wrapped = (z + 1) // chips_z

    def slot(level, q, x_pos, core_pos):
        half = (x_pos % 2 + wrapped) % 2
        return panel.at[level, q, half, (x_pos // 2) * 2 + core_pos]

    def send(level, q, place, send_index, recv_index, device):
        start(remote(place, place, g_send.at[level, q, send_index], g_recv.at[level, q, recv_index], device))

    sources = (x, x_left, x_right, x_far)

    def arrival(level, q, index):
        place = slot(level, q, sources[index % OTHER], core if index < OTHER else 1 - core)
        remote(place, place, g_send.at[level, q, 0], g_recv.at[level, q, index], sibling).wait_recv()
        return place

    send_wrap = 1 - (z + chips_z - 1) // chips_z
    for q in range(CHUNKS):
        start(remote(
            up.at[0, :, pl.ds(q * width, width)], panel.at[0, q, (x_lo + send_wrap) % 2, col],
            g_send.at[0, q, 0], g_recv.at[0, q, 0], below,
        ))

    load_w.wait()
    w_t[...] = w[...].T.reshape(w_t.shape)

    def far_block(way):
        return remote(
            w_t.at[(row + OTHER) % ROWS], far_w.at[way], w_send.at[way], w_recv.at[way], ways[way]
        )

    for way in range(2):
        start(far_block(way))

    def own(q, level=0):
        place = arrival(level, q, 0)
        send(level, q, place, 1, 1, right)
        send(level, q, place, 2, 2, left)
        send(level, q, place, 3, OTHER, sibling)
        if level == 0:
            start(remote(
                place, slot(1, q, x, core), g_send.at[1, q, 0], g_recv.at[1, q, 0], ways[q % 2]
            ))

    def near(q, level=0):
        from_left = arrival(level, q, 1)
        if q % 2 == 0:
            send(level, q, from_left, 7, 3, right)
        send(level, q, from_left, 4, OTHER + 1, sibling)
        from_right = arrival(level, q, 2)
        if q % 2 == 1:
            send(level, q, from_right, 7, 3, left)
        send(level, q, from_right, 5, OTHER + 2, sibling)

    def far(q, level=0):
        place = arrival(level, q, 3)
        send(level, q, place, 6, OTHER + 3, sibling)

    def lines(level, q):
        for index in range(OTHER, 2 * OTHER):
            arrival(level, q, index)
        return jnp.concatenate([panel[level, q, half].reshape(rows, width) for half in range(2)], axis=1)

    def target(way, ahead):
        return (row + (ahead if way == 0 else ROWS - ahead)) % ROWS

    def ring_copy(q, way, half, step):
        return remote(
            part.at[q, target(way, 3 - step), half], arrived.at[q, way, step, half],
            r_send.at[q, way, half, step], r_recv.at[q, way, half, step], ways[way],
        )

    def ring_start(q):
        product = jnp.dot(
            w_t[...].reshape(ROWS * share, rows), lines(0, q), preferred_element_type=jnp.float32
        )
        for half in range(2):
            part[q, :, half] = product[:, half * width:(half + 1) * width].reshape(ROWS, share, width)
        for half in range(2):
            start(ring_copy(q, 1 - q % 2, half, 0))

    def lead_start(q):
        way = q % 2
        if q < 2:
            far_block(way).wait_recv()
        product = jnp.dot(far_w[way], lines(1, q), preferred_element_type=jnp.float32)
        for half in range(2):
            part[q, target(way, 3), half] += product[:, half * width:(half + 1) * width]
            start(ring_copy(q, way, half, 0))

    def ring_step(q, lead, step):
        way = q % 2 if lead else 1 - q % 2
        for half in range(2):
            ring_copy(q, way, half, step).wait_recv()
            if step < 2:
                part[q, target(way, 2 - step), half] += arrived[q, way, step, half]
                start(ring_copy(q, way, half, step + 1))
            elif lead:
                total = part[q, row, half] + arrived[q, 0, 2, half] + arrived[q, 1, 2, half]
                begin = half * tokens + q * width
                ag[0, :, begin:begin + width] = total.astype(ag.dtype)

    def weight_grad(block):
        if block == 0:
            load_a.wait()
        wide = jnp.concatenate(
            [panel[0, q, half, block] for half in range(2) for q in range(CHUNKS)], axis=1
        )
        result = lax.dot_general(
            wide, att[...], (((1,), (1,)), ((), ())), preferred_element_type=jnp.float32
        )
        count = panel.shape[-2]
        wg[0, pl.ds(block * count, count), :] = result.astype(wg.dtype)

    own(0)
    own(1)
    own(2)
    near(0)
    own(3)
    near(1)
    near(2)
    far(0)
    own(0, 1)
    own(1, 1)
    near(3)
    own(2, 1)
    own(3, 1)
    ring_start(0)
    far(1)
    far(2)
    ring_start(1)
    far(3)
    ring_start(2)
    ring_start(3)
    near(0, 1)
    near(1, 1)
    ring_step(0, False, 0)
    ring_step(1, False, 0)
    near(2, 1)
    near(3, 1)
    ring_step(2, False, 0)
    ring_step(3, False, 0)
    weight_grad(0)
    far(0, 1)
    far(1, 1)
    ring_step(0, False, 1)
    ring_step(1, False, 1)
    far(2, 1)
    far(3, 1)
    lead_start(0)
    lead_start(1)
    ring_step(2, False, 1)
    ring_step(3, False, 1)
    lead_start(2)
    lead_start(3)
    for q in range(CHUNKS):
        if q > 0:
            weight_grad(q)
        ring_step(q, False, 2)
    for step in range(3):
        for q in range(CHUNKS):
            ring_step(q, True, step)
    for copy in pending:
        copy.wait_send()


def on_device(chips_z, upstream, attended, weight):
    _, lines, tokens = upstream.shape
    _, features, all_tokens = attended.shape
    _, rows, _ = weight.shape
    share = features // ROWS
    width = tokens // CHUNKS
    bf16 = jnp.bfloat16
    dma = pltpu.SemaphoreType.DMA
    return pl.pallas_call(
        functools.partial(kernel, chips_z),
        out_shape=(
            pltpu.VMEM((1, share, all_tokens), bf16),
            pltpu.VMEM((1, rows, features), bf16),
        ),
        in_specs=[pl.BlockSpec(memory_space=pl.ANY)] * 3,
        out_specs=[pl.BlockSpec(memory_space=pltpu.VMEM)] * 2,
        scratch_shapes=[
            pltpu.VMEM((2, CHUNKS, 2, rows // lines, lines, width), bf16),
            pltpu.VMEM((features, all_tokens), bf16),
            pltpu.VMEM((rows, features), bf16),
            pltpu.VMEM((ROWS, share, rows), bf16),
            pltpu.VMEM((2, share, rows), bf16),
            pltpu.VMEM((CHUNKS, ROWS, 2, share, width), jnp.float32),
            pltpu.VMEM((CHUNKS, 2, 3, 2, share, width), jnp.float32),
            dma((2,)),
            dma((2,)),
            dma((2,)),
            dma((2, CHUNKS, 8)),
            dma((2, CHUNKS, 8)),
            dma((CHUNKS, 2, 2, 3)),
            dma((CHUNKS, 2, 2, 3)),
        ],
        compiler_params=pltpu.CompilerParams(collective_id=0, has_side_effects=True),
    )(upstream, attended, weight)


def solution(mesh):
    placed = (
        P("section", ("row", "col"), None),
        P("section", "col", None),
        P("section", "row", "col"),
    )
    return jax.shard_map(
        functools.partial(on_device, mesh.shape["section"] // 2),
        mesh=mesh,
        in_specs=placed,
        out_specs=(P("section", ("col", "row"), None), P("section", "row", "col")),
        check_vma=False,
    )
```

```python
import functools

import jax
import jax.numpy as jnp
from jax import lax
from jax.experimental import pallas as pl
from jax.experimental.pallas import tpu as pltpu
from jax.sharding import PartitionSpec as P

MESH = pl.DeviceIdType.MESH
CHUNKS = 4
ROWS = 8
DIRECT = (0, 1, 2, 3)
RELAY_LEFT = (1, 3)
OTHER = 4


def kernel(
    chips_z, up, attended, weight, ag, wg,
    panel, att, w, w_t, far_w, part, arrived,
    load_sem, w_send, w_recv, g_send, g_recv, r_send, r_recv,
):
    section, row, col = lax.axis_index("section"), lax.axis_index("row"), lax.axis_index("col")
    x_lo, z = section // chips_z, section % chips_z
    x_hi, core = col // 2, col % 2
    x = 2 * x_hi + x_lo
    width = panel.shape[-1]
    tokens = up.shape[-1]
    share, rows = w_t.shape[1:]

    def at(x_pos, z_pos, core_pos, row_pos):
        return ((x_pos % 2) * chips_z + z_pos, row_pos, (x_pos // 2) * 2 + core_pos)

    x_right, x_left, x_far = (x + 1) % 4, (x + 3) % 4, (x + 2) % 4
    below = at(x, (z + chips_z - 1) % chips_z, core, row)
    above = at(x, (z + 1) % chips_z, core, row)
    beyond = at(x_far, (z + chips_z - 1) % chips_z, core, row)
    before = at(x_far, (z + 1) % chips_z, core, row)
    right, left = at(x_right, z, core, row), at(x_left, z, core, row)
    sibling = at(x, z, 1 - core, row)
    ways = at(x, z, core, (row + 1) % ROWS), at(x, z, core, (row + ROWS - 1) % ROWS)

    barrier = pltpu.get_barrier_semaphore()
    for other in (below, above, beyond, before, right, left, sibling, *ways):
        pl.semaphore_signal(barrier, inc=1, device_id=other, device_id_type=MESH)
    load_w = pltpu.make_async_copy(weight.at[0], w, load_sem.at[0])
    load_a = pltpu.make_async_copy(attended.at[0], att, load_sem.at[1])
    load_w.start()
    load_a.start()
    pl.semaphore_wait(barrier, 9)

    pending = []

    def remote(src, dst, send_sem, recv_sem, device):
        return pltpu.make_async_remote_copy(
            src_ref=src, dst_ref=dst, send_sem=send_sem, recv_sem=recv_sem,
            device_id=device, device_id_type=MESH,
        )

    def start(copy):
        copy.start()
        pending.append(copy)

    wrapped = (z + 1) // chips_z

    def slot(level, q, x_pos, core_pos):
        half = (x_pos % 2 + wrapped) % 2
        return panel.at[level, q, half, (x_pos // 2) * 2 + core_pos]

    def send(level, q, place, send_index, recv_index, device):
        start(remote(place, place, g_send.at[level, q, send_index], g_recv.at[level, q, recv_index], device))

    sources = (x, x_left, x_right, x_far)

    def arrival(level, q, index):
        place = slot(level, q, sources[index % OTHER], core if index < OTHER else 1 - core)
        remote(place, place, g_send.at[level, q, 0], g_recv.at[level, q, index], sibling).wait_recv()
        return place

    send_wrap = 1 - (z + chips_z - 1) // chips_z
    for q in range(CHUNKS):
        chunk = up.at[0, :, pl.ds(q * width, width)]
        place = panel.at[0, q, (x_lo + send_wrap) % 2, col]
        start(remote(chunk, place, g_send.at[0, q, 0], g_recv.at[0, q, 0], below))
        if q in DIRECT:
            start(remote(chunk, place, g_send.at[0, q, 7], g_recv.at[0, q, 3], beyond))

    load_w.wait()
    w_t[...] = w[...].T.reshape(w_t.shape)

    def far_block(way):
        return remote(
            w_t.at[(row + OTHER) % ROWS], far_w.at[way], w_send.at[way], w_recv.at[way], ways[way]
        )

    for way in range(2):
        start(far_block(way))

    half_here = (x_lo + wrapped) % 2
    onward = at(x, z, core, (row + 1 + half_here * (ROWS - 2)) % ROWS)

    def own(q, level=0):
        place = arrival(level, q, 0)
        send(level, q, place, 1, 1, right)
        send(level, q, place, 2, 2, left)
        send(level, q, place, 3, OTHER, sibling)
        if level == 0:
            start(remote(
                place, slot(1, q, x, core), g_send.at[1, q, 0], g_recv.at[1, q, 0], onward
            ))

    def near(q, level=0):
        from_left = arrival(level, q, 1)
        relayed = level > 0 or q not in DIRECT
        if relayed and q not in RELAY_LEFT:
            send(level, q, from_left, 7, 3, right)
        send(level, q, from_left, 4, OTHER + 1, sibling)
        from_right = arrival(level, q, 2)
        if relayed and q in RELAY_LEFT:
            send(level, q, from_right, 7, 3, left)
        send(level, q, from_right, 5, OTHER + 2, sibling)

    def far(q, level=0):
        place = arrival(level, q, 3)
        send(level, q, place, 6, OTHER + 3, sibling)

    def lines(level, q):
        for index in range(OTHER, 2 * OTHER):
            arrival(level, q, index)
        return jnp.concatenate([panel[level, q, half].reshape(rows, width) for half in range(2)], axis=1)

    def target(way, ahead):
        return (row + (ahead if way == 0 else ROWS - ahead)) % ROWS

    def ring_copy(q, way, half, step):
        return remote(
            part.at[q, target(way, 3 - step), half], arrived.at[q, way, step, half],
            r_send.at[q, way, half, step], r_recv.at[q, way, half, step], ways[way],
        )

    def ring_start(q):
        product = jnp.dot(
            w_t[...].reshape(ROWS * share, rows), lines(0, q), preferred_element_type=jnp.float32
        )
        for half in range(2):
            part[q, :, half] = product[:, half * width:(half + 1) * width].reshape(ROWS, share, width)
        for half in range(2):
            start(ring_copy(q, 1 - half, half, 0))

    def lead_start(q):
        both = lines(1, q)
        for half in range(2):
            if q == 0:
                far_block(half).wait_recv()
            product = jnp.dot(
                far_w[half], both[:, half * width:(half + 1) * width], preferred_element_type=jnp.float32
            )
            part[q, target(half, 3), half] += product
            start(ring_copy(q, half, half, 0))

    def ring_step(q, lead, step):
        for half in range(2):
            way = half if lead else 1 - half
            ring_copy(q, way, half, step).wait_recv()
            if step < 2:
                part[q, target(way, 2 - step), half] += arrived[q, way, step, half]
                start(ring_copy(q, way, half, step + 1))
            elif lead:
                total = part[q, row, half] + arrived[q, 0, 2, half] + arrived[q, 1, 2, half]
                begin = half * tokens + q * width
                ag[0, :, begin:begin + width] = total.astype(ag.dtype)

    def weight_grad(block):
        if block == 0:
            load_a.wait()
        wide = jnp.concatenate(
            [panel[0, q, half, block] for half in range(2) for q in range(CHUNKS)], axis=1
        )
        result = lax.dot_general(
            wide, att[...], (((1,), (1,)), ((), ())), preferred_element_type=jnp.float32
        )
        count = panel.shape[-2]
        wg[0, pl.ds(block * count, count), :] = result.astype(wg.dtype)

    own(0)
    own(1)
    far(0)
    near(0)
    own(2)
    far(1)
    ring_start(0)
    near(1)
    own(3)
    far(2)
    ring_start(1)
    near(2)
    own(0, 1)
    own(1, 1)
    far(3)
    ring_start(2)
    near(3)
    own(2, 1)
    own(3, 1)
    ring_start(3)
    near(0, 1)
    near(1, 1)
    ring_step(0, False, 0)
    ring_step(1, False, 0)
    near(2, 1)
    near(3, 1)
    ring_step(2, False, 0)
    ring_step(3, False, 0)
    weight_grad(0)
    far(0, 1)
    far(1, 1)
    ring_step(0, False, 1)
    ring_step(1, False, 1)
    far(2, 1)
    far(3, 1)
    lead_start(0)
    lead_start(1)
    ring_step(2, False, 1)
    ring_step(3, False, 1)
    lead_start(2)
    lead_start(3)
    weight_grad(1)
    ring_step(0, True, 0)
    ring_step(1, True, 0)
    weight_grad(2)
    ring_step(2, True, 0)
    ring_step(3, True, 0)
    weight_grad(3)
    for q in range(CHUNKS):
        ring_step(q, True, 1)
    for q in range(CHUNKS):
        ring_step(q, False, 2)
        ring_step(q, True, 2)
    for copy in pending:
        copy.wait_send()


def on_device(chips_z, upstream, attended, weight):
    _, lines, tokens = upstream.shape
    _, features, all_tokens = attended.shape
    _, rows, _ = weight.shape
    share = features // ROWS
    width = tokens // CHUNKS
    bf16 = jnp.bfloat16
    dma = pltpu.SemaphoreType.DMA
    return pl.pallas_call(
        functools.partial(kernel, chips_z),
        out_shape=(
            pltpu.VMEM((1, share, all_tokens), bf16),
            pltpu.VMEM((1, rows, features), bf16),
        ),
        in_specs=[pl.BlockSpec(memory_space=pl.ANY)] * 3,
        out_specs=[pl.BlockSpec(memory_space=pltpu.VMEM)] * 2,
        scratch_shapes=[
            pltpu.VMEM((2, CHUNKS, 2, rows // lines, lines, width), bf16),
            pltpu.VMEM((features, all_tokens), bf16),
            pltpu.VMEM((rows, features), bf16),
            pltpu.VMEM((ROWS, share, rows), bf16),
            pltpu.VMEM((2, share, rows), bf16),
            pltpu.VMEM((CHUNKS, ROWS, 2, share, width), jnp.float32),
            pltpu.VMEM((CHUNKS, 2, 3, 2, share, width), jnp.float32),
            dma((2,)),
            dma((2,)),
            dma((2,)),
            dma((2, CHUNKS, 8)),
            dma((2, CHUNKS, 8)),
            dma((CHUNKS, 2, 2, 3)),
            dma((CHUNKS, 2, 2, 3)),
        ],
        compiler_params=pltpu.CompilerParams(collective_id=0, has_side_effects=True),
    )(upstream, attended, weight)


def solution(mesh):
    placed = (
        P("section", ("row", "col"), None),
        P("section", "col", None),
        P("section", "row", "col"),
    )
    return jax.shard_map(
        functools.partial(on_device, mesh.shape["section"] // 2),
        mesh=mesh,
        in_specs=placed,
        out_specs=(P("section", ("col", "row"), None), P("section", "row", "col")),
        check_vma=False,
    )
```

```python
import functools

import jax
import jax.numpy as jnp
from jax import lax
from jax.experimental import pallas as pl
from jax.experimental.pallas import tpu as pltpu
from jax.sharding import PartitionSpec as P

MESH = pl.DeviceIdType.MESH
CHUNKS = 4
ROWS = 8
DIRECT = (0, 1, 2, 3)
RELAY_LEFT = (1, 3)
OTHER = 4


def kernel(
    chips_z, up, attended, weight, ag, wg,
    panel, att, w, w_t, far_w, part, arrived,
    load_sem, w_send, w_recv, g_send, g_recv, r_send, r_recv,
):
    section, row, col = lax.axis_index("section"), lax.axis_index("row"), lax.axis_index("col")
    x_lo, z = section // chips_z, section % chips_z
    x_hi, core = col // 2, col % 2
    x = 2 * x_hi + x_lo
    width = panel.shape[-1]
    tokens = up.shape[-1]
    share, rows = w_t.shape[1:]

    def at(x_pos, z_pos, core_pos, row_pos):
        return ((x_pos % 2) * chips_z + z_pos, row_pos, (x_pos // 2) * 2 + core_pos)

    x_right, x_left, x_far = (x + 1) % 4, (x + 3) % 4, (x + 2) % 4
    below = at(x, (z + chips_z - 1) % chips_z, core, row)
    above = at(x, (z + 1) % chips_z, core, row)
    beyond = at(x_far, (z + chips_z - 1) % chips_z, core, row)
    before = at(x_far, (z + 1) % chips_z, core, row)
    right, left = at(x_right, z, core, row), at(x_left, z, core, row)
    sibling = at(x, z, 1 - core, row)
    ways = at(x, z, core, (row + 1) % ROWS), at(x, z, core, (row + ROWS - 1) % ROWS)

    barrier = pltpu.get_barrier_semaphore()
    for other in (below, above, beyond, before, right, left, sibling, *ways):
        pl.semaphore_signal(barrier, inc=1, device_id=other, device_id_type=MESH)
    load_w = pltpu.make_async_copy(weight.at[0], w, load_sem.at[0])
    load_a = pltpu.make_async_copy(attended.at[0], att, load_sem.at[1])
    load_w.start()
    load_a.start()
    pl.semaphore_wait(barrier, 9)

    pending = []

    def remote(src, dst, send_sem, recv_sem, device):
        return pltpu.make_async_remote_copy(
            src_ref=src, dst_ref=dst, send_sem=send_sem, recv_sem=recv_sem,
            device_id=device, device_id_type=MESH,
        )

    def start(copy):
        copy.start()
        pending.append(copy)

    wrapped = (z + 1) // chips_z

    def slot(level, q, x_pos, core_pos):
        half = (x_pos % 2 + wrapped) % 2
        return panel.at[level, q, half, (x_pos // 2) * 2 + core_pos]

    def send(level, q, place, send_index, recv_index, device):
        start(remote(place, place, g_send.at[level, q, send_index], g_recv.at[level, q, recv_index], device))

    sources = (x, x_left, x_right, x_far)

    def arrival(level, q, index):
        place = slot(level, q, sources[index % OTHER], core if index < OTHER else 1 - core)
        remote(place, place, g_send.at[level, q, 0], g_recv.at[level, q, index], sibling).wait_recv()
        return place

    send_wrap = 1 - (z + chips_z - 1) // chips_z
    for q in range(CHUNKS):
        chunk = up.at[0, :, pl.ds(q * width, width)]
        place = panel.at[0, q, (x_lo + send_wrap) % 2, col]
        start(remote(chunk, place, g_send.at[0, q, 0], g_recv.at[0, q, 0], below))
        if q in DIRECT:
            start(remote(chunk, place, g_send.at[0, q, 7], g_recv.at[0, q, 3], beyond))

    load_w.wait()
    w_t[...] = w[...].T.reshape(w_t.shape)

    def far_block(way):
        return remote(
            w_t.at[(row + OTHER) % ROWS], far_w.at[way], w_send.at[way], w_recv.at[way], ways[way]
        )

    for way in range(2):
        start(far_block(way))

    half_here = (x_lo + wrapped) % 2
    onward = at(x, z, core, (row + 1 + half_here * (ROWS - 2)) % ROWS)

    def own(q, level=0):
        place = arrival(level, q, 0)
        send(level, q, place, 1, 1, right)
        send(level, q, place, 2, 2, left)
        send(level, q, place, 3, OTHER, sibling)
        if level == 0:
            start(remote(
                place, slot(1, q, x, core), g_send.at[1, q, 0], g_recv.at[1, q, 0], onward
            ))

    def near(q, level=0):
        from_left = arrival(level, q, 1)
        relayed = level > 0 or q not in DIRECT
        if relayed and q not in RELAY_LEFT:
            send(level, q, from_left, 7, 3, right)
        send(level, q, from_left, 4, OTHER + 1, sibling)
        from_right = arrival(level, q, 2)
        if relayed and q in RELAY_LEFT:
            send(level, q, from_right, 7, 3, left)
        send(level, q, from_right, 5, OTHER + 2, sibling)

    def far(q, level=0):
        place = arrival(level, q, 3)
        send(level, q, place, 6, OTHER + 3, sibling)

    def lines(level, q):
        for index in range(OTHER, 2 * OTHER):
            arrival(level, q, index)
        return jnp.concatenate([panel[level, q, half].reshape(rows, width) for half in range(2)], axis=1)

    def target(way, ahead):
        return (row + (ahead if way == 0 else ROWS - ahead)) % ROWS

    def ring_copy(q, way, half, step):
        return remote(
            part.at[q, target(way, 3 - step), half], arrived.at[q, way, step, half],
            r_send.at[q, way, half, step], r_recv.at[q, way, half, step], ways[way],
        )

    def ring_start(q):
        product = jnp.dot(
            w_t[...].reshape(ROWS * share, rows), lines(0, q), preferred_element_type=jnp.float32
        )
        for half in range(2):
            part[q, :, half] = product[:, half * width:(half + 1) * width].reshape(ROWS, share, width)
        for half in range(2):
            start(ring_copy(q, 1 - half, half, 0))

    def lead_start(q):
        both = lines(1, q)
        for half in range(2):
            if q == 0:
                far_block(half).wait_recv()
            product = jnp.dot(
                far_w[half], both[:, half * width:(half + 1) * width], preferred_element_type=jnp.float32
            )
            part[q, target(half, 3), half] += product
            start(ring_copy(q, half, half, 0))

    def ring_step(q, lead, step):
        for half in range(2):
            way = half if lead else 1 - half
            ring_copy(q, way, half, step).wait_recv()
            if step < 2:
                part[q, target(way, 2 - step), half] += arrived[q, way, step, half]
                start(ring_copy(q, way, half, step + 1))
            elif lead:
                total = part[q, row, half] + arrived[q, 0, 2, half] + arrived[q, 1, 2, half]
                begin = half * tokens + q * width
                ag[0, :, begin:begin + width] = total.astype(ag.dtype)

    def weight_grad(block):
        if block == 0:
            load_a.wait()
        wide = jnp.concatenate(
            [panel[0, q, half, block] for half in range(2) for q in range(CHUNKS)], axis=1
        )
        result = lax.dot_general(
            wide, att[...], (((1,), (1,)), ((), ())), preferred_element_type=jnp.float32
        )
        count = panel.shape[-2]
        wg[0, pl.ds(block * count, count), :] = result.astype(wg.dtype)

    own(0)
    own(1)
    far(0)
    near(0)
    own(2)
    far(1)
    ring_start(0)
    near(1)
    own(3)
    far(2)
    ring_start(1)
    near(2)
    own(0, 1)
    own(1, 1)
    far(3)
    ring_start(2)
    near(3)
    own(2, 1)
    own(3, 1)
    ring_start(3)
    near(0, 1)
    near(1, 1)
    ring_step(0, False, 0)
    ring_step(1, False, 0)
    near(2, 1)
    near(3, 1)
    ring_step(2, False, 0)
    ring_step(3, False, 0)
    weight_grad(0)
    far(0, 1)
    far(1, 1)
    ring_step(0, False, 1)
    ring_step(1, False, 1)
    far(2, 1)
    far(3, 1)
    lead_start(0)
    lead_start(1)
    ring_step(2, False, 1)
    ring_step(3, False, 1)
    lead_start(2)
    lead_start(3)
    weight_grad(1)
    ring_step(0, True, 0)
    ring_step(1, True, 0)
    weight_grad(2)
    ring_step(2, True, 0)
    ring_step(3, True, 0)
    weight_grad(3)
    for q in range(CHUNKS):
        ring_step(q, True, 1)
    for q in range(CHUNKS):
        ring_step(q, False, 2)
        ring_step(q, True, 2)
    for copy in pending:
        copy.wait_send()


def write_out(ag, wg, ag_out, wg_out, sems):
    copies = [
        pltpu.make_async_copy(wg, wg_out, sems.at[0]),
        pltpu.make_async_copy(ag, ag_out, sems.at[1]),
    ]
    for copy in copies:
        copy.start()
    for copy in copies:
        copy.wait()


def on_device(chips_z, upstream, attended, weight):
    _, lines, tokens = upstream.shape
    _, features, all_tokens = attended.shape
    _, rows, _ = weight.shape
    share = features // ROWS
    width = tokens // CHUNKS
    bf16 = jnp.bfloat16
    dma = pltpu.SemaphoreType.DMA
    results = pl.pallas_call(
        functools.partial(kernel, chips_z),
        out_shape=(
            pltpu.VMEM((1, share, all_tokens), bf16),
            pltpu.VMEM((1, rows, features), bf16),
        ),
        in_specs=[pl.BlockSpec(memory_space=pl.ANY)] * 3,
        out_specs=[pl.BlockSpec(memory_space=pltpu.VMEM)] * 2,
        scratch_shapes=[
            pltpu.VMEM((2, CHUNKS, 2, rows // lines, lines, width), bf16),
            pltpu.VMEM((features, all_tokens), bf16),
            pltpu.VMEM((rows, features), bf16),
            pltpu.VMEM((ROWS, share, rows), bf16),
            pltpu.VMEM((2, share, rows), bf16),
            pltpu.VMEM((CHUNKS, ROWS, 2, share, width), jnp.float32),
            pltpu.VMEM((CHUNKS, 2, 3, 2, share, width), jnp.float32),
            dma((2,)),
            dma((2,)),
            dma((2,)),
            dma((2, CHUNKS, 8)),
            dma((2, CHUNKS, 8)),
            dma((CHUNKS, 2, 2, 3)),
            dma((CHUNKS, 2, 2, 3)),
        ],
        compiler_params=pltpu.CompilerParams(collective_id=0, has_side_effects=True),
    )(upstream, attended, weight)
    return pl.pallas_call(
        write_out,
        out_shape=(
            jax.ShapeDtypeStruct((1, share, all_tokens), bf16),
            jax.ShapeDtypeStruct((1, rows, features), bf16),
        ),
        in_specs=[pl.BlockSpec(memory_space=pltpu.VMEM)] * 2,
        out_specs=[pl.BlockSpec(memory_space=pl.ANY)] * 2,
        scratch_shapes=[dma((2,))],
    )(*[pltpu.with_memory_space_constraint(result, pltpu.VMEM) for result in results])


def solution(mesh):
    placed = (
        P("section", ("row", "col"), None),
        P("section", "col", None),
        P("section", "row", "col"),
    )
    return jax.shard_map(
        functools.partial(on_device, mesh.shape["section"] // 2),
        mesh=mesh,
        in_specs=placed,
        out_specs=(P("section", ("col", "row"), None), P("section", "row", "col")),
        check_vma=False,
    )
```
